32 devices in a mesh: groups: 2 (over y), blk: 8 (over z, x), heads: 2 (over core).
Axes of the slice: x: 2, y: 2, z: 4, core: 2. Of those that a mesh axis runs over, the one named last changes fastest.
Arguments:
- queries: bfloat16 [16, 64, 128], P(('groups', 'blk'), 'heads'), parts along dimension 0, may hold values from -256 to 256
- prefix_keys: bfloat16 [4096, 8, 128], P(('groups', 'blk'), 'heads'), parts along dimension 0, may hold values from -12 to 12
- prefix_values: bfloat16 [4096, 8, 128], P(('groups', 'blk'), 'heads'), parts along dimension 0, may hold values from -12 to 12
- suffix_pool: bfloat16 [48, 2, 16, 8, 128], P(('groups', 'blk'), None, None, 'heads'), parts along dimension 0, may hold values from -8.375 to 8.375
- page_owner: int32 [6, 8], P('groups'), parts along dimension 0, may hold values from 0 to 7, as said below
- page_slot: int32 [6, 8], P('groups'), parts along dimension 0, may hold values from 0 to 2, as said below
- suffix_len: int32 [6], P('groups'), parts along dimension 0, may hold values from 1 to 128, as said below
- row_request: int32 [16], P('groups'), parts along dimension 0, may hold values from 0 to 2, as said below
Outputs:
- attn_out: bfloat16 [16, 64, 128], P(('groups', 'blk'), 'heads'), parts along dimension 0
The draws below stay inside these ranges and needn't reach their ends.
There are 2 independent parts, one for each index of `groups`. The reference program is written for one: setup_inputs(seed, part) draws one part's arguments, and reference() takes and returns one part's arrays. A program takes and returns all parts, laid end to end along the dimension named above; each array names one. Nothing has to cross between parts.
Inputs may be any that keep to these rules, and one draw needn't show every extreme that they name: `row_request`: rows 0 to 5 belong to one request, whose last 6 suffix tokens they are, in order; each later row is the only row of its request; every request has rows. `suffix_len`: counts the rows' own tokens; the prefill span's request has 6 or more, and some other request has exactly 128. Each request has one page on every blk index: page j lies on (page_owner[r, 0] + j) modulo the number of blk indices. `page_slot`: A local slot of the owner's pool; two requests never share a slot on one owner.
All inputs are finite; a program needn't handle non-finite values.
Results may differ from the reference program's by a relative error of at most 0.005.
Values may be sent and summed in bfloat16 or wider, within the bound.
A program may use at most 64 MiB of HBM per device.

```python
import math
import jax
import jax.numpy as jnp
from jax import lax

QH = 64
KVH = 8
HD = 128
PAGE = 16
PREFIX = 2048
ROWS = 8
DECODE = 2
SPAN = 6
REQ = 3
SUF_MAX = 128
N_BLK = 8


def key_table(key):
    normal_keys = jnp.clip(jax.random.normal(jax.random.fold_in(key, 11), (PREFIX, KVH, HD), jnp.float32), -5.0, 5.0)
    keys_drawn = normal_keys
    return keys_drawn


def draw_prefix_keys(key, part):
    return key_table(key).astype(jnp.bfloat16)


def draw_queries(key, part):
    drawn = 3.0 * jnp.clip(jax.random.normal(jax.random.fold_in(key, 21), (ROWS, QH, HD), jnp.float32), -6.0, 6.0)
    return drawn.astype(jnp.bfloat16)


def request_tables(key):
    base_key = jax.random.fold_in(key, 31)
    req_order = jax.random.permutation(jax.random.fold_in(base_key, 1), REQ).astype(jnp.int32)
    row_req = jnp.concatenate([jnp.full((SPAN,), req_order[0], jnp.int32), req_order[1:]])
    lengths = jax.random.randint(jax.random.fold_in(base_key, 2), (REQ,), 1, SUF_MAX + 1)
    lengths = lengths.at[req_order[0]].set(jax.random.randint(jax.random.fold_in(base_key, 3), (), SPAN, SUF_MAX + 1))
    longest = req_order[1 + jax.random.randint(jax.random.fold_in(base_key, 4), (), 0, DECODE)]
    lengths = lengths.at[longest].set(SUF_MAX)
    page_count = SUF_MAX // PAGE
    home_owner = jax.random.randint(jax.random.fold_in(base_key, 5), (REQ,), 0, page_count)
    owner_table = (home_owner[:, None] + jnp.arange(page_count)[None, :]) % page_count
    slot_perms = jax.vmap(lambda sub_key: jax.random.permutation(sub_key, REQ))(jax.random.split(jax.random.fold_in(base_key, 6), page_count))
    slot_table = slot_perms[owner_table, jnp.arange(REQ)[:, None]]
    return (row_req.astype(jnp.int32), lengths.astype(jnp.int32), owner_table.astype(jnp.int32), slot_table.astype(jnp.int32))


def draw_row_request(key, part):
    return request_tables(key)[0]


def draw_suffix_len(key, part):
    return request_tables(key)[1]


def draw_page_owner(key, part):
    return request_tables(key)[2]


def draw_page_slot(key, part):
    return request_tables(key)[3]


def levels(key, dims, pieces, low, top_value):
    loudness, own = 1.0, jax.random.fold_in(key, 6)
    for dim, parts in pieces:
        heights = jnp.exp(jax.random.uniform(jax.random.fold_in(own, dim), (parts,), jnp.float32, low / len(pieces), top_value / len(pieces)))
        loudness = loudness * jnp.repeat(heights, dims[dim] // parts).reshape([-1 if axis == dim else 1 for axis in range(len(dims))])
    return loudness


def gaussian(stream_key, dims, width, limit, shards=(), kind=jnp.bfloat16):
    entries = jax.random.normal(stream_key, dims, jnp.float32) * width
    if len(shards) > 0:
        entries = levels(stream_key, dims, shards, -0.22, 0.18) * entries
    return jnp.clip(entries, min=-limit, max=limit).astype(kind)


def setup_inputs(seed: int = 0, part: int = 0) -> dict:
    keys = jax.random.split(jax.random.key(seed), 9)
    part_keys = jax.random.split(jax.random.fold_in(keys[8], part), 9)
    return {
        "queries": draw_queries(jax.random.fold_in(jax.random.fold_in(keys[8], part), 71), part),
        "prefix_keys": draw_prefix_keys(jax.random.fold_in(jax.random.fold_in(keys[8], part), 71), part),
        "prefix_values": gaussian(part_keys[2], (PREFIX, KVH, HD), 2.0, 12.0, ((0, 8), (1, 2))),
        "suffix_pool": gaussian(part_keys[3], (REQ * N_BLK, 2, PAGE, KVH, HD), 1.4, 8.375, ((0, 8), (3, 2))),
        "page_owner": draw_page_owner(jax.random.fold_in(jax.random.fold_in(keys[8], part), 71), part),
        "page_slot": draw_page_slot(jax.random.fold_in(jax.random.fold_in(keys[8], part), 71), part),
        "suffix_len": draw_suffix_len(jax.random.fold_in(jax.random.fold_in(keys[8], part), 71), part),
        "row_request": draw_row_request(jax.random.fold_in(jax.random.fold_in(keys[8], part), 71), part),
    }


def reference(queries, prefix_keys, prefix_values, suffix_pool, page_owner, page_slot, suffix_len, row_request):
    group = QH // KVH
    score_scale = 1.0 / math.sqrt(HD)
    keys_wide = prefix_keys.astype(jnp.float32)
    values_wide = prefix_values.astype(jnp.float32)
    pool_rows = (page_owner * REQ + page_slot).astype(jnp.int32)
    row_order = jnp.arange(ROWS, dtype=jnp.int32)
    same_req = row_request[:, None] == row_request[None, :]
    later_rows = lax.optimization_barrier(jnp.sum((same_req & (row_order[None, :] > row_order[:, None])).astype(jnp.int32), axis=1))
    limits = (suffix_len[row_request] - later_rows).astype(jnp.int32)
    token_pos = jnp.arange(SUF_MAX, dtype=jnp.int32)

    def one_row(packed):
        query_row, request, row_limit = packed
        grouped = query_row.astype(jnp.float32).reshape(KVH, group, HD)
        page_data = suffix_pool[pool_rows[request]].astype(jnp.float32)
        suffix_keys = page_data[:, 0].reshape(SUF_MAX, KVH, HD)
        suffix_values = page_data[:, 1].reshape(SUF_MAX, KVH, HD)
        prefix_scores = jnp.einsum('gqd,kgd->gqk', grouped, keys_wide) * score_scale
        suffix_scores = jnp.einsum('gqd,kgd->gqk', grouped, suffix_keys) * score_scale
        visible = token_pos < row_limit
        highest = jnp.maximum(lax.optimization_barrier(jnp.max(prefix_scores, axis=-1)), lax.optimization_barrier(jnp.max(jnp.where(visible, suffix_scores, -jnp.inf), axis=-1)))
        prefix_probs = jnp.exp(prefix_scores - highest[..., None])
        suffix_probs = jnp.where(visible, jnp.exp(suffix_scores - highest[..., None]), 0.0)
        denominator = lax.optimization_barrier(jnp.sum(prefix_probs, axis=-1)) + lax.optimization_barrier(jnp.sum(suffix_probs, axis=-1))
        rounded_prefix = lax.optimization_barrier(prefix_probs.astype(jnp.bfloat16)).astype(jnp.float32)
        rounded_suffix = lax.optimization_barrier(suffix_probs.astype(jnp.bfloat16)).astype(jnp.float32)
        mixed = jnp.einsum('gqk,kgd->gqd', rounded_prefix, values_wide)
        mixed = mixed + jnp.einsum('gqk,kgd->gqd', rounded_suffix, suffix_values)
        return (mixed / denominator[..., None]).reshape(QH, HD).astype(jnp.bfloat16)
    return lax.map(one_row, (queries, row_request, limits))
```

```python
import functools
import math

import jax
import jax.numpy as jnp
from jax import lax
from jax.experimental import pallas as pl
from jax.experimental.pallas import tpu as pltpu
from jax.sharding import PartitionSpec as P

MESH = pl.DeviceIdType.MESH
MASKED = -1e30
LANES = 128


def repeat(count, body, limit=16):
    if count <= limit:
        for step in range(count):
            body(step)
    else:

        def wrapped(step, carry):
            body(step)
            return carry

        lax.fori_loop(0, count, wrapped, 0)


def kernel(
    dims,
    q_ref,
    keys_ref,
    values_ref,
    pool_ref,
    owner_ref,
    slot_ref,
    len_ref,
    request_ref,
    out_ref,
    q_all,
    k_all,
    v_all,
    o_send,
    s_send,
    o_recv,
    s_recv,
    load_sem,
    q_send_sem,
    q_recv_sem,
    o_send_sem,
    o_recv_sem,
    s_send_sem,
    s_recv_sem,
):
    n, rows_dev, heads, head_dim, kv_heads, page_len, slots, chunk = dims
    rows = n * rows_dev
    group = heads // kv_heads
    page_rows = page_len * kv_heads
    prefix_rows = keys_ref.shape[0]
    total_rows = k_all.shape[0]
    suffix_rows = total_rows - prefix_rows
    exp_scale = math.log2(math.e) / math.sqrt(head_dim)
    me = lax.axis_index("blk")

    def peer(k):
        return lax.rem(me + k + 1, n)

    barrier = pltpu.get_barrier_semaphore()
    repeat(
        n - 1,
        lambda k: pl.semaphore_signal(
            barrier, inc=1, device_id={"blk": peer(k)}, device_id_type=MESH
        ),
    )

    own_rows = pl.ds(me * rows_dev, rows_dev)
    own_q = pltpu.make_async_copy(q_ref, q_all.at[own_rows], load_sem.at[0])
    own_q.start()
    prefix_k = pltpu.make_async_copy(keys_ref, k_all.at[pl.ds(0, prefix_rows)], load_sem.at[1])
    prefix_k.start()
    prefix_v = pltpu.make_async_copy(values_ref, v_all.at[pl.ds(0, prefix_rows)], load_sem.at[2])
    prefix_v.start()

    def page_copies(s):
        place = pl.ds(prefix_rows + s * page_rows, page_rows)
        return (
            pltpu.make_async_copy(
                pool_ref.at[pl.ds(2 * s * page_rows, page_rows)],
                k_all.at[place],
                load_sem.at[3 + 2 * s],
            ),
            pltpu.make_async_copy(
                pool_ref.at[pl.ds((2 * s + 1) * page_rows, page_rows)],
                v_all.at[place],
                load_sem.at[4 + 2 * s],
            ),
        )

    def start_page(s):
        for copy in page_copies(s):
            copy.start()

    def wait_page(s):
        for copy in page_copies(s):
            copy.wait()

    repeat(slots, start_page)
    used = prefix_rows + slots * page_rows
    if used < total_rows:
        pad = jnp.zeros((total_rows - used, head_dim), jnp.bfloat16)
        k_all[used:, :] = pad
        v_all[used:, :] = pad

    pl.semaphore_wait(barrier, n - 1)

    def query_copy(k, source):
        return pltpu.make_async_remote_copy(
            src_ref=q_ref,
            dst_ref=q_all.at[pl.ds(source * rows_dev, rows_dev)],
            send_sem=q_send_sem.at[k],
            recv_sem=q_recv_sem.at[source],
            device_id={"blk": peer(k)},
            device_id_type=MESH,
        )

    repeat(n - 1, lambda k: query_copy(k, me).start())

    def row_range(row):
        request = request_ref[row]
        later = jnp.int32(0)
        if rows <= 16:
            for other in range(rows):
                if isinstance(row, int) and other <= row:
                    continue
                later = later + jnp.where(
                    jnp.logical_and(request_ref[other] == request, other > row), 1, 0
                )
        else:
            later = lax.fori_loop(
                0,
                rows,
                lambda other, count: count
                + jnp.where(jnp.logical_and(request_ref[other] == request, other > row), 1, 0),
                later,
            )
        page = lax.rem(me - owner_ref[request, 0] + n, n)
        shown = len_ref[request] - later - page * page_len
        shown = jnp.minimum(jnp.maximum(shown, 0), page_len)
        low = slot_ref[request, page] * page_rows
        return low, low + shown * kv_heads

    head_of = lax.broadcasted_iota(jnp.int32, (heads, LANES), 0) // group
    lane = lax.broadcasted_iota(jnp.int32, (heads, LANES), 1)
    same = lax.rem(lane, kv_heads) == head_of
    head_ok = jnp.concatenate([same] * (total_rows // LANES), axis=1)
    suffix_ok = head_ok[:, prefix_rows:]
    column = lax.broadcasted_iota(jnp.int32, (heads, suffix_rows), 1)

    def row_mask(row):
        low, high = row_range(row)
        seen = jnp.logical_and(column >= low, column < high)
        return jnp.logical_and(seen, suffix_ok)

    prefix_k.wait()
    prefix_v.wait()
    repeat(slots, wait_page)
    own_q.wait()
    repeat(n - 1, lambda k: query_copy(k, peer(k)).wait_recv())

    def chunk_step(c):
        first = c * chunk
        q = q_all[pl.ds(first, chunk)].reshape(chunk * heads, head_dim)
        scores = lax.dot_general(
            q, k_all[...], (((1,), (1,)), ((), ())), preferred_element_type=jnp.float32
        )
        blocks = []
        for r in range(chunk):
            block = scores[r * heads : (r + 1) * heads]
            blocks.append(
                jnp.concatenate(
                    [
                        jnp.where(head_ok[:, :prefix_rows], block[:, :prefix_rows], MASKED),
                        jnp.where(row_mask(first + r), block[:, prefix_rows:], MASKED),
                    ],
                    axis=1,
                )
            )
        scores = jnp.concatenate(blocks, axis=0)
        highest = jnp.max(scores, axis=1, keepdims=True)
        probs = jnp.exp2((scores - highest) * exp_scale)
        total = jnp.sum(probs, axis=1, keepdims=True)
        mixed = jnp.dot(
            probs.astype(jnp.bfloat16), v_all[...], preferred_element_type=jnp.float32
        )
        o_send[pl.ds(first, chunk)] = (
            (mixed / total).astype(jnp.bfloat16).reshape(chunk, heads, head_dim)
        )
        wide = lax.broadcasted_iota(jnp.int32, (chunk * heads, LANES), 1)
        stats = jnp.where(wide == 0, highest, total).T
        for r in range(chunk):
            s_send[first + r, :, 0:heads] = stats[0:2, r * heads : (r + 1) * heads]

    repeat(rows // chunk, chunk_step, 1)

    def o_copy(k, target, source):
        return pltpu.make_async_remote_copy(
            src_ref=o_send.at[pl.ds(target * rows_dev, rows_dev)],
            dst_ref=o_recv.at[source],
            send_sem=o_send_sem.at[k],
            recv_sem=o_recv_sem.at[source],
            device_id={"blk": peer(k)},
            device_id_type=MESH,
        )

    def s_copy(k, target, source):
        return pltpu.make_async_remote_copy(
            src_ref=s_send.at[pl.ds(target * rows_dev, rows_dev)],
            dst_ref=s_recv.at[source],
            send_sem=s_send_sem.at[k],
            recv_sem=s_recv_sem.at[source],
            device_id={"blk": peer(k)},
            device_id_type=MESH,
        )

    def send(k):
        s_copy(k, peer(k), me).start()
        o_copy(k, peer(k), me).start()

    repeat(n - 1, send)
    o_recv[me] = o_send[own_rows]
    s_recv[me] = s_send[own_rows]

    def receive(k):
        s_copy(k, me, peer(k)).wait_recv()
        o_copy(k, me, peer(k)).wait_recv()

    repeat(n - 1, receive)

    for r in range(rows_dev):
        tops = s_recv[:, r, 0, :]
        sums = s_recv[:, r, 1, :]
        top = jnp.max(tops, axis=0, keepdims=True)
        weights = sums * jnp.exp2((tops - top) * exp_scale)
        weights = weights / jnp.sum(weights, axis=0, keepdims=True)
        columns = weights.T
        merged = jnp.zeros((heads, head_dim), jnp.float32)
        for p in range(n):
            merged = merged + o_recv[p, r].astype(jnp.float32) * columns[0:heads, p : p + 1]
        out_ref[r] = merged.astype(out_ref.dtype)

    def finish(k):
        query_copy(k, me).wait_send()
        s_copy(k, peer(k), me).wait_send()
        o_copy(k, peer(k), me).wait_send()

    repeat(n - 1, finish)


def on_device(
    queries, prefix_keys, prefix_values, suffix_pool, page_owner, page_slot, suffix_len, row_request
):
    n = lax.axis_size("blk")
    rows_dev, heads, head_dim = queries.shape
    kv_heads = prefix_keys.shape[1]
    slots, _, page_len = suffix_pool.shape[:3]
    rows = n * rows_dev
    chunk = math.gcd(rows, 8)
    prefix_rows = prefix_keys.shape[0] * kv_heads
    suffix_rows = -(-slots * page_len * kv_heads // LANES) * LANES
    total_rows = prefix_rows + suffix_rows
    dims = (n, rows_dev, heads, head_dim, kv_heads, page_len, slots, chunk)
    anywhere = pl.BlockSpec(memory_space=pl.ANY)
    scalar = pl.BlockSpec(memory_space=pltpu.SMEM)
    bf16, f32 = jnp.bfloat16, jnp.float32
    dma = pltpu.SemaphoreType.DMA
    return pl.pallas_call(
        functools.partial(kernel, dims),
        out_shape=jax.ShapeDtypeStruct(queries.shape, queries.dtype),
        in_specs=[anywhere] * 4 + [scalar] * 4,
        out_specs=pl.BlockSpec(memory_space=pltpu.VMEM),
        scratch_shapes=[
            pltpu.VMEM((rows, heads, head_dim), bf16),
            pltpu.VMEM((total_rows, head_dim), bf16),
            pltpu.VMEM((total_rows, head_dim), bf16),
            pltpu.VMEM((rows, heads, head_dim), bf16),
            pltpu.VMEM((rows, 2, LANES), f32),
            pltpu.VMEM((n, rows_dev, heads, head_dim), bf16),
            pltpu.VMEM((n, rows_dev, 2, LANES), f32),
            dma((3 + 2 * slots,)),
            dma((n - 1,)),
            dma((n,)),
            dma((n - 1,)),
            dma((n,)),
            dma((n - 1,)),
            dma((n,)),
        ],
        compiler_params=pltpu.CompilerParams(collective_id=0, has_side_effects=True),
    )(
        queries,
        prefix_keys.reshape(prefix_rows, head_dim),
        prefix_values.reshape(prefix_rows, head_dim),
        suffix_pool.reshape(slots * 2 * page_len * kv_heads, head_dim),
        page_owner,
        page_slot,
        suffix_len,
        row_request,
    )


def solution(mesh):
    placed = (
        P(("groups", "blk"), "heads", None),
        P(("groups", "blk"), "heads", None),
        P(("groups", "blk"), "heads", None),
        P(("groups", "blk"), None, None, "heads", None),
        P("groups", None),
        P("groups", None),
        P("groups"),
        P("groups"),
    )
    return jax.shard_map(
        on_device,
        mesh=mesh,
        in_specs=placed,
        out_specs=P(("groups", "blk"), "heads", None),
        check_vma=False,
    )
```

```python
import functools
import math

import jax
import jax.numpy as jnp
from jax import lax
from jax.experimental import pallas as pl
from jax.experimental.pallas import tpu as pltpu
from jax.sharding import PartitionSpec as P

MESH = pl.DeviceIdType.MESH
MASKED = -1e30
LANES = 128


def repeat(count, body, limit=16):
    if count <= limit:
        for step in range(count):
            body(step)
    else:

        def wrapped(step, carry):
            body(step)
            return carry

        lax.fori_loop(0, count, wrapped, 0)


def kernel(
    dims,
    q_ref,
    keys_ref,
    values_ref,
    pool_ref,
    owner_hbm,
    slot_hbm,
    len_hbm,
    request_hbm,
    out_ref,
    owner_ref,
    slot_ref,
    len_ref,
    request_ref,
    q_all,
    k_all,
    v_all,
    o_send,
    s_send,
    o_recv,
    s_recv,
    load_sem,
    table_sem,
    q_send_sem,
    q_recv_sem,
    o_send_sem,
    o_recv_sem,
    s_send_sem,
    s_recv_sem,
):
    n, rows_dev, heads, head_dim, kv_heads, page_len, slots, chunk = dims
    rows = n * rows_dev
    group = heads // kv_heads
    page_rows = page_len * kv_heads
    prefix_rows = keys_ref.shape[0]
    total_rows = k_all.shape[0]
    suffix_rows = total_rows - prefix_rows
    exp_scale = math.log2(math.e) / math.sqrt(head_dim)
    me = lax.axis_index("blk")

    def peer(k):
        return lax.rem(me + k + 1, n)

    barrier = pltpu.get_barrier_semaphore()
    repeat(
        n - 1,
        lambda k: pl.semaphore_signal(
            barrier, inc=1, device_id={"blk": peer(k)}, device_id_type=MESH
        ),
    )

    tables = [
        pltpu.make_async_copy(source, place, table_sem.at[i])
        for i, (source, place) in enumerate(
            (
                (owner_hbm, owner_ref),
                (slot_hbm, slot_ref),
                (len_hbm, len_ref),
                (request_hbm, request_ref),
            )
        )
    ]
    for table in tables:
        table.start()
    own_rows = pl.ds(me * rows_dev, rows_dev)
    own_q = pltpu.make_async_copy(q_ref, q_all.at[own_rows], load_sem.at[0])
    own_q.start()
    prefix_k = pltpu.make_async_copy(keys_ref, k_all.at[pl.ds(0, prefix_rows)], load_sem.at[1])
    prefix_k.start()
    prefix_v = pltpu.make_async_copy(values_ref, v_all.at[pl.ds(0, prefix_rows)], load_sem.at[2])
    prefix_v.start()

    def page_copies(s):
        place = pl.ds(prefix_rows + s * page_rows, page_rows)
        return (
            pltpu.make_async_copy(
                pool_ref.at[pl.ds(2 * s * page_rows, page_rows)],
                k_all.at[place],
                load_sem.at[3 + 2 * s],
            ),
            pltpu.make_async_copy(
                pool_ref.at[pl.ds((2 * s + 1) * page_rows, page_rows)],
                v_all.at[place],
                load_sem.at[4 + 2 * s],
            ),
        )

    def start_page(s):
        for copy in page_copies(s):
            copy.start()

    def wait_page(s):
        for copy in page_copies(s):
            copy.wait()

    repeat(slots, start_page)
    used = prefix_rows + slots * page_rows
    if used < total_rows:
        pad = jnp.zeros((total_rows - used, head_dim), jnp.bfloat16)
        k_all[used:, :] = pad
        v_all[used:, :] = pad

    pl.semaphore_wait(barrier, n - 1)

    def query_copy(k, source):
        return pltpu.make_async_remote_copy(
            src_ref=q_ref,
            dst_ref=q_all.at[pl.ds(source * rows_dev, rows_dev)],
            send_sem=q_send_sem.at[k],
            recv_sem=q_recv_sem.at[source],
            device_id={"blk": peer(k)},
            device_id_type=MESH,
        )

    repeat(n - 1, lambda k: query_copy(k, me).start())

    def row_range(row):
        request = request_ref[row]
        later = jnp.int32(0)
        if rows <= 16:
            for other in range(rows):
                if isinstance(row, int) and other <= row:
                    continue
                later = later + jnp.where(
                    jnp.logical_and(request_ref[other] == request, other > row), 1, 0
                )
        else:
            later = lax.fori_loop(
                0,
                rows,
                lambda other, count: count
                + jnp.where(jnp.logical_and(request_ref[other] == request, other > row), 1, 0),
                later,
            )
        page = lax.rem(me - owner_ref[request, 0] + n, n)
        shown = len_ref[request] - later - page * page_len
        shown = jnp.minimum(jnp.maximum(shown, 0), page_len)
        low = slot_ref[request, page] * page_rows
        return low, low + shown * kv_heads

    head_of = lax.broadcasted_iota(jnp.int32, (heads, LANES), 0) // group
    lane = lax.broadcasted_iota(jnp.int32, (heads, LANES), 1)
    same = lax.rem(lane, kv_heads) == head_of
    head_ok = jnp.concatenate([same] * (total_rows // LANES), axis=1)
    suffix_ok = head_ok[:, prefix_rows:]
    column = lax.broadcasted_iota(jnp.int32, (heads, suffix_rows), 1)

    def row_mask(row):
        low, high = row_range(row)
        seen = jnp.logical_and(column >= low, column < high)
        return jnp.logical_and(seen, suffix_ok)

    for table in tables:
        table.wait()
    prefix_k.wait()
    prefix_v.wait()
    repeat(slots, wait_page)
    own_q.wait()
    repeat(n - 1, lambda k: query_copy(k, peer(k)).wait_recv())

    def chunk_step(c):
        first = c * chunk
        q = q_all[pl.ds(first, chunk)].reshape(chunk * heads, head_dim)
        scores = lax.dot_general(
            q, k_all[...], (((1,), (1,)), ((), ())), preferred_element_type=jnp.float32
        )
        blocks = []
        for r in range(chunk):
            block = scores[r * heads : (r + 1) * heads]
            blocks.append(
                jnp.concatenate(
                    [
                        jnp.where(head_ok[:, :prefix_rows], block[:, :prefix_rows], MASKED),
                        jnp.where(row_mask(first + r), block[:, prefix_rows:], MASKED),
                    ],
                    axis=1,
                )
            )
        scores = jnp.concatenate(blocks, axis=0)
        highest = jnp.max(scores, axis=1, keepdims=True)
        probs = jnp.exp2((scores - highest) * exp_scale)
        total = jnp.sum(probs, axis=1, keepdims=True)
        mixed = jnp.dot(
            probs.astype(jnp.bfloat16), v_all[...], preferred_element_type=jnp.float32
        )
        o_send[pl.ds(first, chunk)] = mixed.reshape(chunk, heads, head_dim)
        wide = lax.broadcasted_iota(jnp.int32, (chunk * heads, LANES), 1)
        stats = jnp.where(wide == 0, highest, total).T
        for r in range(chunk):
            s_send[first + r, :, 0:heads] = stats[0:2, r * heads : (r + 1) * heads]

    repeat(rows // chunk, chunk_step, 1)

    def o_copy(k, target, source):
        return pltpu.make_async_remote_copy(
            src_ref=o_send.at[pl.ds(target * rows_dev, rows_dev)],
            dst_ref=o_recv.at[source],
            send_sem=o_send_sem.at[k],
            recv_sem=o_recv_sem.at[source],
            device_id={"blk": peer(k)},
            device_id_type=MESH,
        )

    def s_copy(k, target, source):
        return pltpu.make_async_remote_copy(
            src_ref=s_send.at[pl.ds(target * rows_dev, rows_dev)],
            dst_ref=s_recv.at[source],
            send_sem=s_send_sem.at[k],
            recv_sem=s_recv_sem.at[source],
            device_id={"blk": peer(k)},
            device_id_type=MESH,
        )

    def send(k):
        s_copy(k, peer(k), me).start()
        o_copy(k, peer(k), me).start()

    repeat(n - 1, send)
    o_recv[me] = o_send[own_rows]
    s_recv[me] = s_send[own_rows]

    def receive(k):
        s_copy(k, me, peer(k)).wait_recv()
        o_copy(k, me, peer(k)).wait_recv()

    repeat(n - 1, receive)

    for r in range(rows_dev):
        tops = s_recv[:, r, 0, :]
        sums = s_recv[:, r, 1, :]
        top = jnp.max(tops, axis=0, keepdims=True)
        weights = jnp.exp2((tops - top) * exp_scale)
        weights = weights / jnp.sum(weights * sums, axis=0, keepdims=True)
        columns = weights.T
        merged = jnp.zeros((heads, head_dim), jnp.float32)
        for p in range(n):
            merged = merged + o_recv[p, r] * columns[0:heads, p : p + 1]
        out_ref[r] = merged.astype(out_ref.dtype)

    def finish(k):
        query_copy(k, me).wait_send()
        s_copy(k, peer(k), me).wait_send()
        o_copy(k, peer(k), me).wait_send()

    repeat(n - 1, finish)


def on_device(
    queries, prefix_keys, prefix_values, suffix_pool, page_owner, page_slot, suffix_len, row_request
):
    n = lax.axis_size("blk")
    rows_dev, heads, head_dim = queries.shape
    kv_heads = prefix_keys.shape[1]
    slots, _, page_len = suffix_pool.shape[:3]
    rows = n * rows_dev
    chunk = math.gcd(rows, 8)
    prefix_rows = prefix_keys.shape[0] * kv_heads
    suffix_rows = -(-slots * page_len * kv_heads // LANES) * LANES
    total_rows = prefix_rows + suffix_rows
    dims = (n, rows_dev, heads, head_dim, kv_heads, page_len, slots, chunk)
    anywhere = pl.BlockSpec(memory_space=pl.ANY)
    bf16, f32 = jnp.bfloat16, jnp.float32
    dma = pltpu.SemaphoreType.DMA
    return pl.pallas_call(
        functools.partial(kernel, dims),
        out_shape=pltpu.VMEM(queries.shape, queries.dtype),
        in_specs=[anywhere] * 8,
        out_specs=pl.BlockSpec(memory_space=pltpu.VMEM),
        scratch_shapes=[
            pltpu.SMEM(page_owner.shape, jnp.int32),
            pltpu.SMEM(page_slot.shape, jnp.int32),
            pltpu.SMEM(suffix_len.shape, jnp.int32),
            pltpu.SMEM(row_request.shape, jnp.int32),
            pltpu.VMEM((rows, heads, head_dim), bf16),
            pltpu.VMEM((total_rows, head_dim), bf16),
            pltpu.VMEM((total_rows, head_dim), bf16),
            pltpu.VMEM((rows, heads, head_dim), f32),
            pltpu.VMEM((rows, 2, LANES), f32),
            pltpu.VMEM((n, rows_dev, heads, head_dim), f32),
            pltpu.VMEM((n, rows_dev, 2, LANES), f32),
            dma((3 + 2 * slots,)),
            dma((4,)),
            dma((n - 1,)),
            dma((n,)),
            dma((n - 1,)),
            dma((n,)),
            dma((n - 1,)),
            dma((n,)),
        ],
        compiler_params=pltpu.CompilerParams(collective_id=0, has_side_effects=True),
    )(
        queries,
        prefix_keys.reshape(prefix_rows, head_dim),
        prefix_values.reshape(prefix_rows, head_dim),
        suffix_pool.reshape(slots * 2 * page_len * kv_heads, head_dim),
        page_owner,
        page_slot,
        suffix_len,
        row_request,
    )


def solution(mesh):
    placed = (
        P(("groups", "blk"), "heads", None),
        P(("groups", "blk"), "heads", None),
        P(("groups", "blk"), "heads", None),
        P(("groups", "blk"), None, None, "heads", None),
        P("groups", None),
        P("groups", None),
        P("groups"),
        P("groups"),
    )
    return jax.shard_map(
        on_device,
        mesh=mesh,
        in_specs=placed,
        out_specs=P(("groups", "blk"), "heads", None),
        check_vma=False,
    )
```

```python
import functools
import math

import jax
import jax.numpy as jnp
from jax import lax
from jax.experimental import pallas as pl
from jax.experimental.pallas import tpu as pltpu
from jax.sharding import PartitionSpec as P

MESH = pl.DeviceIdType.MESH
MASKED = -1e30
LANES = 128


def repeat(count, body, limit=16):
    if count <= limit:
        for step in range(count):
            body(step)
    else:

        def wrapped(step, carry):
            body(step)
            return carry

        lax.fori_loop(0, count, wrapped, 0)


def kernel(
    dims,
    q_ref,
    keys_ref,
    values_ref,
    pool_ref,
    owner_hbm,
    slot_hbm,
    len_hbm,
    request_hbm,
    out_ref,
    owner_ref,
    slot_ref,
    len_ref,
    request_ref,
    head_bias,
    row_bias,
    q_all,
    k_all,
    v_all,
    o_send,
    s_send,
    o_recv,
    s_recv,
    load_sem,
    table_sem,
    q_send_sem,
    q_recv_sem,
    o_send_sem,
    o_recv_sem,
    s_send_sem,
    s_recv_sem,
):
    n, rows_dev, heads, head_dim, kv_heads, page_len, slots, chunk = dims
    rows = n * rows_dev
    group = heads // kv_heads
    page_rows = page_len * kv_heads
    prefix_rows = keys_ref.shape[0]
    total_rows = k_all.shape[0]
    suffix_rows = total_rows - prefix_rows
    exp_scale = math.log2(math.e) / math.sqrt(head_dim)
    me = lax.axis_index("blk")

    half = n // 2
    side = me // half
    local = me - side * half

    def far_peer(k):
        return n - 1 - side * half - lax.rem(local + k, half)

    def near_peer(k):
        return side * half + lax.rem(local + k + 1, half)

    def far_peers(body):
        repeat(half, lambda k: body(k, far_peer(k)))

    def near_peers(body):
        repeat(half - 1, lambda k: body(half + k, near_peer(k)))

    barrier = pltpu.get_barrier_semaphore()

    def greet(k, peer):
        pl.semaphore_signal(barrier, inc=1, device_id={"blk": peer}, device_id_type=MESH)

    far_peers(greet)
    near_peers(greet)

    tables = [
        pltpu.make_async_copy(source, place, table_sem.at[i])
        for i, (source, place) in enumerate(
            (
                (owner_hbm, owner_ref),
                (slot_hbm, slot_ref),
                (len_hbm, len_ref),
                (request_hbm, request_ref),
            )
        )
    ]
    for table in tables:
        table.start()
    own_rows = pl.ds(me * rows_dev, rows_dev)
    own_q = pltpu.make_async_copy(q_ref, q_all.at[own_rows], load_sem.at[0])
    own_q.start()
    prefix_k = pltpu.make_async_copy(keys_ref, k_all.at[pl.ds(0, prefix_rows)], load_sem.at[1])
    prefix_k.start()
    prefix_v = pltpu.make_async_copy(values_ref, v_all.at[pl.ds(0, prefix_rows)], load_sem.at[2])
    prefix_v.start()

    def page_copies(s):
        place = pl.ds(prefix_rows + s * page_rows, page_rows)
        return (
            pltpu.make_async_copy(
                pool_ref.at[pl.ds(2 * s * page_rows, page_rows)],
                k_all.at[place],
                load_sem.at[3 + 2 * s],
            ),
            pltpu.make_async_copy(
                pool_ref.at[pl.ds((2 * s + 1) * page_rows, page_rows)],
                v_all.at[place],
                load_sem.at[4 + 2 * s],
            ),
        )

    def start_page(s):
        for copy in page_copies(s):
            copy.start()

    def wait_page(s):
        for copy in page_copies(s):
            copy.wait()

    repeat(slots, start_page)
    own_q.wait()
    pl.semaphore_wait(barrier, n - 1)

    def query_copy(k, peer, source):
        return pltpu.make_async_remote_copy(
            src_ref=q_all.at[own_rows],
            dst_ref=q_all.at[pl.ds(source * rows_dev, rows_dev)],
            send_sem=q_send_sem.at[k],
            recv_sem=q_recv_sem.at[source],
            device_id={"blk": peer},
            device_id_type=MESH,
        )

    far_peers(lambda k, peer: query_copy(k, peer, me).start())
    near_peers(lambda k, peer: query_copy(k, peer, me).start())

    used = prefix_rows + slots * page_rows
    if used < total_rows:
        pad = jnp.zeros((total_rows - used, head_dim), jnp.bfloat16)
        k_all[used:, :] = pad
        v_all[used:, :] = pad

    def row_range(row):
        request = request_ref[row]
        later = jnp.int32(0)
        if rows <= 16:
            for other in range(rows):
                if isinstance(row, int) and other <= row:
                    continue
                later = later + jnp.where(
                    jnp.logical_and(request_ref[other] == request, other > row), 1, 0
                )
        else:
            later = lax.fori_loop(
                0,
                rows,
                lambda other, count: count
                + jnp.where(jnp.logical_and(request_ref[other] == request, other > row), 1, 0),
                later,
            )
        page = lax.rem(me - owner_ref[request, 0] + n, n)
        shown = len_ref[request] - later - page * page_len
        shown = jnp.minimum(jnp.maximum(shown, 0), page_len)
        low = slot_ref[request, page] * page_rows
        return low, low + shown * kv_heads

    head_of = lax.broadcasted_iota(jnp.int32, (heads, LANES), 0) // group
    lane = lax.broadcasted_iota(jnp.int32, (heads, LANES), 1)
    head_tile = jnp.where(lax.rem(lane, kv_heads) == head_of, 0.0, MASKED)
    for place in range(0, total_rows, LANES):
        head_bias[:, place : place + LANES] = head_tile
    column = lax.broadcasted_iota(jnp.int32, (1, suffix_rows), 1)
    for table in tables:
        table.wait()

    def set_row_bias(row):
        low, high = row_range(row)
        seen = jnp.logical_and(column >= low, column < high)
        row_bias[row] = jnp.where(seen, 0.0, MASKED)

    repeat(rows, set_row_bias)
    prefix_k.wait()
    prefix_v.wait()
    repeat(slots, wait_page)

    def chunk_step(first):
        q = q_all[pl.ds(first, chunk)].reshape(chunk * heads, head_dim)
        scores = lax.dot_general(
            q, k_all[...], (((1,), (1,)), ((), ())), preferred_element_type=jnp.float32
        )
        blocks = []
        for r in range(chunk):
            block = scores[r * heads : (r + 1) * heads] + head_bias[...]
            blocks.append(
                jnp.concatenate(
                    [block[:, :prefix_rows], block[:, prefix_rows:] + row_bias[first + r]], axis=1
                )
            )
        scores = jnp.concatenate(blocks, axis=0)
        highest = jnp.max(scores, axis=1, keepdims=True)
        probs = jnp.exp2((scores - highest) * exp_scale)
        total = jnp.sum(probs, axis=1, keepdims=True)
        mixed = jnp.dot(
            probs.astype(jnp.bfloat16), v_all[...], preferred_element_type=jnp.float32
        )
        o_send[pl.ds(first, chunk)] = mixed.reshape(chunk, heads, head_dim)
        wide = lax.broadcasted_iota(jnp.int32, (chunk * heads, LANES), 1)
        stats = jnp.where(wide == 0, highest, total).T
        for r in range(chunk):
            s_send[first + r, :, 0:heads] = stats[0:2, r * heads : (r + 1) * heads]

    def o_copy(k, peer, target, source):
        return pltpu.make_async_remote_copy(
            src_ref=o_send.at[pl.ds(target * rows_dev, rows_dev)],
            dst_ref=o_recv.at[source],
            send_sem=o_send_sem.at[k],
            recv_sem=o_recv_sem.at[source],
            device_id={"blk": peer},
            device_id_type=MESH,
        )

    def s_copy(k, peer, target, source):
        return pltpu.make_async_remote_copy(
            src_ref=s_send.at[pl.ds(target * rows_dev, rows_dev)],
            dst_ref=s_recv.at[source],
            send_sem=s_send_sem.at[k],
            recv_sem=s_recv_sem.at[source],
            device_id={"blk": peer},
            device_id_type=MESH,
        )

    def send(k, peer):
        s_copy(k, peer, peer, me).start()
        o_copy(k, peer, peer, me).start()

    def attend(which):
        first = which * half * rows_dev
        repeat(half * rows_dev // chunk, lambda c: chunk_step(first + c * chunk), 1)

    near_peers(lambda k, peer: query_copy(k, peer, peer).wait_recv())
    attend(side)
    near_peers(send)
    o_recv[me] = o_send[own_rows]
    s_recv[me] = s_send[own_rows]
    far_peers(lambda k, peer: query_copy(k, peer, peer).wait_recv())
    attend(1 - side)
    far_peers(send)

    def receive(k, peer):
        s_copy(k, peer, me, peer).wait_recv()
        o_copy(k, peer, me, peer).wait_recv()

    near_peers(receive)
    far_peers(receive)

    for r in range(rows_dev):
        tops = s_recv[:, r, 0, :]
        sums = s_recv[:, r, 1, :]
        top = jnp.max(tops, axis=0, keepdims=True)
        weights = jnp.exp2((tops - top) * exp_scale)
        weights = weights / jnp.sum(weights * sums, axis=0, keepdims=True)
        columns = weights.T
        merged = jnp.zeros((heads, head_dim), jnp.float32)
        for p in range(n):
            merged = merged + o_recv[p, r] * columns[0:heads, p : p + 1]
        out_ref[r] = merged.astype(out_ref.dtype)

    def finish(k, peer):
        query_copy(k, peer, me).wait_send()
        s_copy(k, peer, peer, me).wait_send()
        o_copy(k, peer, peer, me).wait_send()

    far_peers(finish)
    near_peers(finish)


def on_device(
    queries, prefix_keys, prefix_values, suffix_pool, page_owner, page_slot, suffix_len, row_request
):
    n = lax.axis_size("blk")
    rows_dev, heads, head_dim = queries.shape
    kv_heads = prefix_keys.shape[1]
    slots, _, page_len = suffix_pool.shape[:3]
    rows = n * rows_dev
    chunk = math.gcd(rows // 2, 4)
    prefix_rows = prefix_keys.shape[0] * kv_heads
    suffix_rows = -(-slots * page_len * kv_heads // LANES) * LANES
    total_rows = prefix_rows + suffix_rows
    dims = (n, rows_dev, heads, head_dim, kv_heads, page_len, slots, chunk)
    anywhere = pl.BlockSpec(memory_space=pl.ANY)
    bf16, f32 = jnp.bfloat16, jnp.float32
    dma = pltpu.SemaphoreType.DMA
    return pl.pallas_call(
        functools.partial(kernel, dims),
        out_shape=pltpu.VMEM(queries.shape, queries.dtype),
        in_specs=[anywhere] * 8,
        out_specs=pl.BlockSpec(memory_space=pltpu.VMEM),
        scratch_shapes=[
            pltpu.SMEM(page_owner.shape, jnp.int32),
            pltpu.SMEM(page_slot.shape, jnp.int32),
            pltpu.SMEM(suffix_len.shape, jnp.int32),
            pltpu.SMEM(row_request.shape, jnp.int32),
            pltpu.VMEM((heads, total_rows), f32),
            pltpu.VMEM((rows, 1, suffix_rows), f32),
            pltpu.VMEM((rows, heads, head_dim), bf16),
            pltpu.VMEM((total_rows, head_dim), bf16),
            pltpu.VMEM((total_rows, head_dim), bf16),
            pltpu.VMEM((rows, heads, head_dim), f32),
            pltpu.VMEM((rows, 2, LANES), f32),
            pltpu.VMEM((n, rows_dev, heads, head_dim), f32),
            pltpu.VMEM((n, rows_dev, 2, LANES), f32),
            dma((3 + 2 * slots,)),
            dma((4,)),
            dma((n - 1,)),
            dma((n,)),
            dma((n - 1,)),
            dma((n,)),
            dma((n - 1,)),
            dma((n,)),
        ],
        compiler_params=pltpu.CompilerParams(collective_id=0, has_side_effects=True),
    )(
        queries,
        prefix_keys.reshape(prefix_rows, head_dim),
        prefix_values.reshape(prefix_rows, head_dim),
        suffix_pool.reshape(slots * 2 * page_len * kv_heads, head_dim),
        page_owner,
        page_slot,
        suffix_len,
        row_request,
    )


def solution(mesh):
    placed = (
        P(("groups", "blk"), "heads", None),
        P(("groups", "blk"), "heads", None),
        P(("groups", "blk"), "heads", None),
        P(("groups", "blk"), None, None, "heads", None),
        P("groups", None),
        P("groups", None),
        P("groups"),
        P("groups"),
    )
    return jax.shard_map(
        on_device,
        mesh=mesh,
        in_specs=placed,
        out_specs=P(("groups", "blk"), "heads", None),
        check_vma=False,
    )
```

```python
import functools
import math

import jax
import jax.numpy as jnp
from jax import lax
from jax.experimental import pallas as pl
from jax.experimental.pallas import tpu as pltpu
from jax.sharding import PartitionSpec as P

MESH = pl.DeviceIdType.MESH
MASKED = -1e30
LANES = 128


def repeat(count, body, limit=16):
    if count <= limit:
        for step in range(count):
            body(step)
    else:

        def wrapped(step, carry):
            body(step)
            return carry

        lax.fori_loop(0, count, wrapped, 0)


def kernel(
    dims,
    q_ref,
    keys_ref,
    values_ref,
    pool_ref,
    owner_hbm,
    slot_hbm,
    len_hbm,
    request_hbm,
    out_ref,
    owner_ref,
    slot_ref,
    len_ref,
    request_ref,
    head_bias,
    row_bias,
    q_all,
    k_all,
    v_all,
    o_send,
    s_send,
    o_recv,
    s_recv,
    load_sem,
    table_sem,
    q_send_sem,
    q_recv_sem,
    o_send_sem,
    o_recv_sem,
    s_send_sem,
    s_recv_sem,
):
    n, rows_dev, heads, head_dim, kv_heads, page_len, slots, chunk = dims
    rows = n * rows_dev
    group = heads // kv_heads
    page_rows = page_len * kv_heads
    prefix_rows = keys_ref.shape[0]
    total_rows = k_all.shape[0]
    suffix_rows = total_rows - prefix_rows
    exp_scale = math.log2(math.e) / math.sqrt(head_dim)
    me = lax.axis_index("blk")

    half = n // 2
    side = me // half
    local = me - side * half

    def far_peer(k):
        return n - 1 - side * half - lax.rem(local + k, half)

    def near_peer(k):
        return side * half + lax.rem(local + half - 1 - k, half)

    def far_peers(body):
        repeat(half, lambda k: body(k, far_peer(k)))

    def near_peers(body):
        repeat(half - 1, lambda k: body(half + k, near_peer(k)))

    barrier = pltpu.get_barrier_semaphore()

    def greet(k, peer):
        pl.semaphore_signal(barrier, inc=1, device_id={"blk": peer}, device_id_type=MESH)

    far_peers(greet)
    near_peers(greet)

    tables = [
        pltpu.make_async_copy(source, place, table_sem.at[i])
        for i, (source, place) in enumerate(
            (
                (owner_hbm, owner_ref),
                (slot_hbm, slot_ref),
                (len_hbm, len_ref),
                (request_hbm, request_ref),
            )
        )
    ]
    for table in tables:
        table.start()
    own_rows = pl.ds(me * rows_dev, rows_dev)
    own_q = pltpu.make_async_copy(q_ref, q_all.at[own_rows], load_sem.at[0])
    own_q.start()
    prefix_k = pltpu.make_async_copy(keys_ref, k_all.at[pl.ds(0, prefix_rows)], load_sem.at[1])
    prefix_k.start()
    prefix_v = pltpu.make_async_copy(values_ref, v_all.at[pl.ds(0, prefix_rows)], load_sem.at[2])
    prefix_v.start()

    def page_copies(s):
        place = pl.ds(prefix_rows + s * page_rows, page_rows)
        return (
            pltpu.make_async_copy(
                pool_ref.at[pl.ds(2 * s * page_rows, page_rows)],
                k_all.at[place],
                load_sem.at[3 + 2 * s],
            ),
            pltpu.make_async_copy(
                pool_ref.at[pl.ds((2 * s + 1) * page_rows, page_rows)],
                v_all.at[place],
                load_sem.at[4 + 2 * s],
            ),
        )

    def start_page(s):
        for copy in page_copies(s):
            copy.start()

    def wait_page(s):
        for copy in page_copies(s):
            copy.wait()

    repeat(slots, start_page)
    own_q.wait()
    pl.semaphore_wait(barrier, n - 1)

    def query_copy(k, peer, source):
        return pltpu.make_async_remote_copy(
            src_ref=q_all.at[own_rows],
            dst_ref=q_all.at[pl.ds(source * rows_dev, rows_dev)],
            send_sem=q_send_sem.at[k],
            recv_sem=q_recv_sem.at[source],
            device_id={"blk": peer},
            device_id_type=MESH,
        )

    far_peers(lambda k, peer: query_copy(k, peer, me).start())
    near_peers(lambda k, peer: query_copy(k, peer, me).start())

    used = prefix_rows + slots * page_rows
    if used < total_rows:
        pad = jnp.zeros((total_rows - used, head_dim), jnp.bfloat16)
        k_all[used:, :] = pad
        v_all[used:, :] = pad

    def row_range(row):
        request = request_ref[row]
        later = jnp.int32(0)
        if rows <= 16:
            for other in range(rows):
                if isinstance(row, int) and other <= row:
                    continue
                later = later + jnp.where(
                    jnp.logical_and(request_ref[other] == request, other > row), 1, 0
                )
        else:
            later = lax.fori_loop(
                0,
                rows,
                lambda other, count: count
                + jnp.where(jnp.logical_and(request_ref[other] == request, other > row), 1, 0),
                later,
            )
        page = lax.rem(me - owner_ref[request, 0] + n, n)
        shown = len_ref[request] - later - page * page_len
        shown = jnp.minimum(jnp.maximum(shown, 0), page_len)
        low = slot_ref[request, page] * page_rows
        return low, low + shown * kv_heads

    head_of = lax.broadcasted_iota(jnp.int32, (heads, LANES), 0) // group
    lane = lax.broadcasted_iota(jnp.int32, (heads, LANES), 1)
    head_tile = jnp.where(lax.rem(lane, kv_heads) == head_of, 0.0, MASKED)
    for place in range(0, total_rows, LANES):
        head_bias[:, place : place + LANES] = head_tile
    column = lax.broadcasted_iota(jnp.int32, (1, suffix_rows), 1)
    for table in tables:
        table.wait()

    def set_row_bias(row):
        low, high = row_range(row)
        seen = jnp.logical_and(column >= low, column < high)
        row_bias[row] = jnp.where(seen, 0.0, MASKED)

    repeat(rows, set_row_bias)
    prefix_k.wait()
    prefix_v.wait()
    repeat(slots, wait_page)

    def chunk_step(first):
        q = q_all[pl.ds(first, chunk)].reshape(chunk * heads, head_dim)
        scores = lax.dot_general(
            q, k_all[...], (((1,), (1,)), ((), ())), preferred_element_type=jnp.float32
        )
        blocks = []
        for r in range(chunk):
            block = scores[r * heads : (r + 1) * heads] + head_bias[...]
            blocks.append(
                jnp.concatenate(
                    [block[:, :prefix_rows], block[:, prefix_rows:] + row_bias[first + r]], axis=1
                )
            )
        scores = jnp.concatenate(blocks, axis=0)
        highest = jnp.max(scores, axis=1, keepdims=True)
        probs = jnp.exp2((scores - highest) * exp_scale)
        total = jnp.sum(probs, axis=1, keepdims=True)
        mixed = jnp.dot(
            probs.astype(jnp.bfloat16), v_all[...], preferred_element_type=jnp.float32
        )
        o_send[pl.ds(first, chunk)] = mixed.reshape(chunk, heads, head_dim)
        wide = lax.broadcasted_iota(jnp.int32, (chunk * heads, LANES), 1)
        stats = jnp.where(wide == 0, highest, total).T
        for r in range(chunk):
            s_send[first + r, :, 0:heads] = stats[0:2, r * heads : (r + 1) * heads]

    def o_copy(k, peer, target, source):
        return pltpu.make_async_remote_copy(
            src_ref=o_send.at[pl.ds(target * rows_dev, rows_dev)],
            dst_ref=o_recv.at[source],
            send_sem=o_send_sem.at[k],
            recv_sem=o_recv_sem.at[source],
            device_id={"blk": peer},
            device_id_type=MESH,
        )

    def s_copy(k, peer, target, source):
        return pltpu.make_async_remote_copy(
            src_ref=s_send.at[pl.ds(target * rows_dev, rows_dev)],
            dst_ref=s_recv.at[source],
            send_sem=s_send_sem.at[k],
            recv_sem=s_recv_sem.at[source],
            device_id={"blk": peer},
            device_id_type=MESH,
        )

    def send(k, peer):
        s_copy(k, peer, peer, me).start()
        o_copy(k, peer, peer, me).start()

    def attend(which):
        first = which * half * rows_dev
        repeat(half * rows_dev // chunk, lambda c: chunk_step(first + c * chunk), 1)

    near_peers(lambda k, peer: query_copy(k, peer, peer).wait_recv())
    attend(side)
    near_peers(send)
    far_peers(lambda k, peer: query_copy(k, peer, peer).wait_recv())
    attend(1 - side)
    far_peers(send)
    o_recv[me] = o_send[own_rows]
    s_recv[me] = s_send[own_rows]

    def receive(k, peer):
        s_copy(k, peer, me, peer).wait_recv()
        o_copy(k, peer, me, peer).wait_recv()

    near_peers(receive)
    far_peers(receive)

    for r in range(rows_dev):
        tops = s_recv[:, r, 0, :]
        sums = s_recv[:, r, 1, :]
        top = jnp.max(tops, axis=0, keepdims=True)
        weights = jnp.exp2((tops - top) * exp_scale)
        weights = weights / jnp.sum(weights * sums, axis=0, keepdims=True)
        columns = weights.T
        merged = jnp.zeros((heads, head_dim), jnp.float32)
        for p in range(n):
            merged = merged + o_recv[p, r] * columns[0:heads, p : p + 1]
        out_ref[r] = merged.astype(out_ref.dtype)

    def finish(k, peer):
        query_copy(k, peer, me).wait_send()
        s_copy(k, peer, peer, me).wait_send()
        o_copy(k, peer, peer, me).wait_send()

    far_peers(finish)
    near_peers(finish)


def on_device(
    queries, prefix_keys, prefix_values, suffix_pool, page_owner, page_slot, suffix_len, row_request
):
    n = lax.axis_size("blk")
    rows_dev, heads, head_dim = queries.shape
    kv_heads = prefix_keys.shape[1]
    slots, _, page_len = suffix_pool.shape[:3]
    rows = n * rows_dev
    chunk = math.gcd(rows // 2, 4)
    prefix_rows = prefix_keys.shape[0] * kv_heads
    suffix_rows = -(-slots * page_len * kv_heads // LANES) * LANES
    total_rows = prefix_rows + suffix_rows
    dims = (n, rows_dev, heads, head_dim, kv_heads, page_len, slots, chunk)
    anywhere = pl.BlockSpec(memory_space=pl.ANY)
    bf16, f32 = jnp.bfloat16, jnp.float32
    dma = pltpu.SemaphoreType.DMA
    return pl.pallas_call(
        functools.partial(kernel, dims),
        out_shape=pltpu.VMEM(queries.shape, queries.dtype),
        in_specs=[anywhere] * 8,
        out_specs=pl.BlockSpec(memory_space=pltpu.VMEM),
        scratch_shapes=[
            pltpu.SMEM(page_owner.shape, jnp.int32),
            pltpu.SMEM(page_slot.shape, jnp.int32),
            pltpu.SMEM(suffix_len.shape, jnp.int32),
            pltpu.SMEM(row_request.shape, jnp.int32),
            pltpu.VMEM((heads, total_rows), f32),
            pltpu.VMEM((rows, 1, suffix_rows), f32),
            pltpu.VMEM((rows, heads, head_dim), bf16),
            pltpu.VMEM((total_rows, head_dim), bf16),
            pltpu.VMEM((total_rows, head_dim), bf16),
            pltpu.VMEM((rows, heads, head_dim), f32),
            pltpu.VMEM((rows, 2, LANES), f32),
            pltpu.VMEM((n, rows_dev, heads, head_dim), f32),
            pltpu.VMEM((n, rows_dev, 2, LANES), f32),
            dma((3 + 2 * slots,)),
            dma((4,)),
            dma((n - 1,)),
            dma((n,)),
            dma((n - 1,)),
            dma((n,)),
            dma((n - 1,)),
            dma((n,)),
        ],
        compiler_params=pltpu.CompilerParams(collective_id=0, has_side_effects=True),
    )(
        queries,
        prefix_keys.reshape(prefix_rows, head_dim),
        prefix_values.reshape(prefix_rows, head_dim),
        suffix_pool.reshape(slots * 2 * page_len * kv_heads, head_dim),
        page_owner,
        page_slot,
        suffix_len,
        row_request,
    )


def solution(mesh):
    placed = (
        P(("groups", "blk"), "heads", None),
        P(("groups", "blk"), "heads", None),
        P(("groups", "blk"), "heads", None),
        P(("groups", "blk"), None, None, "heads", None),
        P("groups", None),
        P("groups", None),
        P("groups"),
        P("groups"),
    )
    return jax.shard_map(
        on_device,
        mesh=mesh,
        in_specs=placed,
        out_specs=P(("groups", "blk"), "heads", None),
        check_vma=False,
    )
```
